32 devices in a mesh: inp: 8 (over z, x), tm: 4 (over y, core).
Axes of the slice: x: 2, y: 2, z: 4, core: 2. Of those that a mesh axis runs over, the one named last changes fastest.
Arguments:
- samples: bfloat16 [576, 2, 24576], P('inp', None, 'tm'), may hold values from -6 to 6
- delays: int32 [576], P('inp'), may hold values from 0 to 3840
- taps: int32 [16, 256], replicated, may hold values from -2048 to 2047
Outputs:
- visibilities: float32 [256, 576, 1152], P('inp', 'tm')
The draws below stay inside these ranges and needn't reach their ends.
All inputs are finite; a program needn't handle non-finite values.
Results may differ from the reference program's by a relative error of at most 0.0031.
Values may be sent and summed in bfloat16 or wider, within the bound.
A program may use at most 128 MiB of HBM per device.

```python
import math
import jax
import jax.numpy as jnp
from jax import lax

INPUTS = 576
CH = 256
TAPS = 16
NT = 24576
HALO = 3840


def place_ends(drawn, stream_key, smallest, largest):
    index_at = [jax.random.randint(jax.random.fold_in(stream_key, axis), (), 0, length) for axis, length in enumerate(drawn.shape)]
    main_axis = drawn.shape.index(max(drawn.shape))
    next_to = index_at[:main_axis] + [(index_at[main_axis] + 1) % drawn.shape[main_axis]] + index_at[main_axis + 1:]
    return drawn.at[tuple(index_at)].set(smallest).at[tuple(next_to)].set(largest)


def steps_of(own_key, shape, split, smallest, top_value):
    def one(position, blocks):
        draws = jax.random.uniform(jax.random.fold_in(jax.random.fold_in(own_key, 6), position), (blocks,), jnp.float32, smallest / len(split), top_value / len(split))
        return jnp.repeat(jnp.exp(draws), shape[position] // blocks).reshape((-1,) + (1,) * (len(shape) - position - 1))

    level = one(*split[0])
    for cut in split[1:]:
        level = level * one(*cut)
    return level


def centred(own_key, shape, width, bound, cuts=(), kind=jnp.bfloat16):
    drawn = width * jax.random.normal(own_key, shape, jnp.float32)
    if cuts:
        drawn = drawn * steps_of(own_key, shape, cuts, -0.22, 0.18)
    return jnp.clip(drawn, -bound, bound).astype(kind)


def setup_inputs(seed: int = 0) -> dict:
    arg_keys = jax.random.split(jax.random.key(seed), 4)
    return {
        "samples": centred(arg_keys[0], (INPUTS, 2, NT), 1.0, 6.0, ((0, 8), (2, 4))),
        "delays": place_ends(jax.random.randint(arg_keys[1], (INPUTS,), 0, HALO + 1), jax.random.fold_in(arg_keys[1], 1), 0, HALO).astype(jnp.int32),
        "taps": place_ends(jax.random.randint(arg_keys[2], (TAPS, CH), -2048, 2048), jax.random.fold_in(arg_keys[2], 1), -2048, 2047).astype(jnp.int32),
    }


def dft_table(length):
    channel_index = jnp.arange(length, dtype=jnp.int32)
    phase = (jnp.outer(channel_index, channel_index) % length).astype(jnp.float32) * (2.0 * math.pi / length)
    cosine = jnp.cos(phase)
    sine = jnp.sin(phase)
    upper = jnp.concatenate([cosine, -sine], axis=1)
    lower = jnp.concatenate([sine, cosine], axis=1)
    return jnp.concatenate([upper, lower], axis=0) / math.sqrt(length)

def reference(samples, delays, taps):
    coefficient = taps.astype(jnp.float32) * (1.0 / 4096.0)
    table = dft_table(CH)
    count = NT // CH

    def one_input(operands):
        series, offset = operands
        values = series.astype(jnp.float32)
        aligned = jnp.roll(values, -offset, axis=1)
        frames = aligned.reshape(2, count, CH)
        filtered = jnp.zeros_like(frames)
        for tap in range(TAPS):
            filtered = filtered + coefficient[tap][None, None, :] * jnp.roll(frames, tap, axis=1)
        stacked = jnp.concatenate([filtered[0], filtered[1]], axis=1)
        spectrum = jnp.dot(stacked, table, precision=lax.Precision.HIGHEST)
        return spectrum.astype(jnp.bfloat16)
    spectra = lax.map(one_input, (samples, delays.astype(jnp.int32)))
    by_channel = jnp.transpose(spectra, (2, 0, 1))

    def one_channel(operands):
        real_part, imag_part = operands
        row_block = jnp.concatenate([real_part, imag_part], axis=1)
        swapped = jnp.concatenate([imag_part, -real_part], axis=1)
        gram_real = jnp.dot(row_block, row_block.T, preferred_element_type=jnp.float32)
        gram_imag = jnp.dot(swapped, row_block.T, preferred_element_type=jnp.float32)
        return jnp.concatenate([gram_real, gram_imag], axis=1) * (1.0 / count)
    return lax.map(one_channel, (by_channel[:CH], by_channel[CH:]))
```

```python
import functools
import math

import jax
import jax.numpy as jnp
import numpy as np
from jax import lax
from jax.experimental import pallas as pl
from jax.experimental.pallas import tpu as pltpu
from jax.sharding import PartitionSpec as P

LANES = 128
GROUP = 8


def dft_tables(length, groups):
    index = np.arange(length)
    phase = (np.outer(index, index) % length) * (2.0 * math.pi / length)
    cosine, sine = np.cos(phase), np.sin(phase)
    table = np.stack([np.stack([cosine, -sine]), np.stack([sine, cosine])])
    table = table.transpose(0, 2, 1, 3).reshape(2 * length, 2, groups, length // groups)
    table = table.transpose(0, 2, 1, 3).reshape(2 * length, 2 * length) / math.sqrt(length)
    high = table.astype(jnp.bfloat16)
    low = (table - high.astype(np.float64)).astype(jnp.bfloat16)
    return high, low


def spectra_kernel(dims, delays_ref, before_ref, own_ref, after_ref, coef_ref, high_ref, low_ref, out_ref, flat, slab, filt):
    tap_count, parts, spectra, hist, skip = dims
    own = own_ref.shape[2]
    groups = out_ref.shape[0]
    frames = spectra + tap_count - 1
    need = -(-frames * parts // GROUP) * GROUP
    step = pl.program_id(0)
    lane = lax.broadcasted_iota(jnp.int32, (need, LANES), 1)
    for c in range(2):
        for j in range(GROUP):
            delay = delays_ref[step * GROUP + j]
            rows, shift = delay // LANES, delay % LANES
            turn = lax.rem(LANES - shift, LANES)
            buf = flat.at[(c * GROUP + j) % flat.shape[0]]
            buf[0:hist, :] = pltpu.roll(before_ref[j, c].astype(jnp.float32), turn, 1)
            buf[hist : hist + own, :] = pltpu.roll(own_ref[j, c].astype(jnp.float32), turn, 1)
            buf[hist + own : hist + own + hist, :] = pltpu.roll(after_ref[j, c].astype(jnp.float32), turn, 1)
            low = buf[pl.ds(rows + skip, need), :]
            high = buf[pl.ds(rows + skip + 1, need), :]
            slab[c, pl.ds(j, need, stride=GROUP), :] = jnp.where(lane < LANES - shift, low, high)
    block = 8
    for c in range(2):
        for h in range(parts):
            for s0 in range(0, spectra, block):
                taps = [coef_ref[m, h] for m in range(tap_count)]
                held = {}
                for s in range(s0, min(s0 + block, spectra)):
                    total = None
                    for m in range(tap_count):
                        row = parts * (s + tap_count - 1 - m) + h
                        if row not in held:
                            held[row] = slab[c, row * GROUP : (row + 1) * GROUP, :]
                        term = taps[m] * held[row]
                        total = term if total is None else total + term
                    filt[s * GROUP : (s + 1) * GROUP, (c * parts + h) * LANES : (c * parts + h + 1) * LANES] = total
    value = filt[...]
    high = value.astype(jnp.bfloat16)
    low = (value - high.astype(jnp.float32)).astype(jnp.bfloat16)
    result = (
        jnp.dot(high, high_ref[...], preferred_element_type=jnp.float32)
        + jnp.dot(low, high_ref[...], preferred_element_type=jnp.float32)
        + jnp.dot(high, low_ref[...], preferred_element_type=jnp.float32)
    )
    width = result.shape[1] // groups
    packs = LANES // width
    rows = spectra * GROUP // packs
    place = lax.broadcasted_iota(jnp.int32, (rows, LANES), 1) // width
    for p in range(groups // packs):
        pieces = [result[j * rows : (j + 1) * rows, p * LANES : (p + 1) * LANES] for j in range(packs)]
        for q in range(packs):
            total = pieces[q]
            for j in range(packs):
                if j != q:
                    moved = pltpu.roll(pieces[j], ((j - q) * width) % LANES, 1)
                    total = jnp.where(place == j, moved, total)
            out_ref[p * packs + q, 0] = total.astype(jnp.bfloat16)


def gram_kernel(scale, which_ref, x_ref, out_ref, mine):
    shards, _, depth, inputs = x_ref.shape
    rows = out_ref.shape[1]
    half = depth // 2
    x = x_ref[...].reshape(shards * depth, inputs)
    for t in range(inputs // rows):

        @pl.when(which_ref[0] == t)
        def _():
            mine[...] = x[:, t * rows : (t + 1) * rows].astype(jnp.float32)

    left = mine[...]
    turned = []
    for t in range(shards):
        turned.append(left[t * depth + half : (t + 1) * depth])
        turned.append(-left[t * depth : t * depth + half])
    turned = jnp.concatenate(turned, axis=0).astype(jnp.bfloat16)
    dims = (((0,), (0,)), ((), ()))
    real = lax.dot_general(left.astype(jnp.bfloat16), x, dims, preferred_element_type=jnp.float32)
    imag = lax.dot_general(turned, x, dims, preferred_element_type=jnp.float32)
    out_ref[0, :, 0:inputs] = real * scale
    out_ref[0, :, inputs : 2 * inputs] = imag * scale


def front(samples, delays, taps):
    tap_count, channels = taps.shape
    local_inputs, _, shard_len = samples.shape
    peers = lax.axis_size("tm")
    groups = lax.axis_size("inp")
    parts = channels // LANES
    spectra = shard_len // channels
    margin_rows = (tap_count - 1) * parts
    hist = -(-margin_rows // 16) * 16
    own = shard_len // LANES
    lined = samples.reshape(local_inputs, 2, own, LANES)
    up = [(i, (i + 1) % peers) for i in range(peers)]
    down = [(j, i) for i, j in up]
    before = lax.ppermute(lined[:, :, own - hist :], "tm", up)
    after = lax.ppermute(lined[:, :, :hist], "tm", down)
    steps = -(-local_inputs // GROUP)
    offsets = jnp.pad(delays, (0, steps * GROUP - local_inputs))
    coef = (taps.astype(jnp.float32) * (1.0 / 4096.0)).reshape(tap_count, parts, 1, LANES)
    coef = jnp.broadcast_to(coef, (tap_count, parts, GROUP, LANES))
    high, low = dft_tables(channels, groups)
    width = 2 * channels // groups
    packs = LANES // width
    rows = spectra * GROUP // packs
    need = -(-(spectra + tap_count - 1) * parts // GROUP) * GROUP
    total = -(-max(2 * hist + own, need + hist + 1) // GROUP) * GROUP
    fixed = lambda shape: pl.BlockSpec(shape, lambda i, d: (0,) * len(shape))
    return pl.pallas_call(
        functools.partial(spectra_kernel, (tap_count, parts, spectra, hist, hist - margin_rows)),
        out_shape=jax.ShapeDtypeStruct((groups, steps, rows, LANES), jnp.bfloat16),
        grid_spec=pltpu.PrefetchScalarGridSpec(
            num_scalar_prefetch=1,
            grid=(steps,),
            in_specs=[
                pl.BlockSpec((GROUP, 2, hist, LANES), lambda i, d: (i, 0, 0, 0)),
                pl.BlockSpec((GROUP, 2, own, LANES), lambda i, d: (i, 0, 0, 0)),
                pl.BlockSpec((GROUP, 2, hist, LANES), lambda i, d: (i, 0, 0, 0)),
                fixed(coef.shape),
                fixed(high.shape),
                fixed(low.shape),
            ],
            out_specs=pl.BlockSpec((groups, 1, rows, LANES), lambda i, d: (0, i, 0, 0)),
            scratch_shapes=[
                pltpu.VMEM((4, total, LANES), jnp.float32),
                pltpu.VMEM((2, need * GROUP, LANES), jnp.float32),
                pltpu.VMEM((spectra * GROUP, 2 * channels), jnp.float32),
            ],
        ),
        name="spectra",
    )(offsets, before, lined, after, coef, jnp.asarray(high), jnp.asarray(low))


def gram(gathered, rows, scale):
    shards, channels, depth, inputs = gathered.shape
    which = lax.axis_index("tm").astype(jnp.int32).reshape(1)
    return pl.pallas_call(
        functools.partial(gram_kernel, scale),
        out_shape=jax.ShapeDtypeStruct((channels, rows, 2 * inputs), jnp.float32),
        grid_spec=pltpu.PrefetchScalarGridSpec(
            num_scalar_prefetch=1,
            grid=(channels,),
            in_specs=[pl.BlockSpec((shards, 1, depth, inputs), lambda f, w: (0, f, 0, 0))],
            out_specs=pl.BlockSpec((1, rows, 2 * inputs), lambda f, w: (f, 0, 0)),
            scratch_shapes=[pltpu.VMEM((shards * depth, rows), jnp.float32)],
        ),
        name="gram",
    )(which, gathered)


def shards(samples, delays, taps):
    channels = taps.shape[1]
    local_inputs, _, shard_len = samples.shape
    groups, peers = lax.axis_size("inp"), lax.axis_size("tm")
    inputs = local_inputs * groups
    spectra = shard_len // channels
    mine = channels // groups
    packs = LANES // (2 * mine)
    sent = front(samples, delays, taps)
    turned = lax.all_to_all(sent, "inp", split_axis=0, concat_axis=0, tiled=True)
    steps = turned.shape[1]
    turned = turned.reshape(groups, steps, spectra // packs, GROUP, packs, 2, mine)
    turned = turned.transpose(6, 5, 4, 2, 0, 1, 3).reshape(mine, 2 * spectra, groups, steps * GROUP)
    turned = turned[..., :local_inputs].reshape(mine, 2 * spectra, inputs)
    gathered = lax.all_gather(turned, "tm", axis=0, tiled=False)
    return gram(gathered, inputs // peers, 1.0 / (spectra * peers))


def solution(mesh):
    in_specs = (P("inp", None, "tm"), P("inp"), P())
    out_specs = P("inp", "tm", None)
    return jax.shard_map(shards, mesh=mesh, in_specs=in_specs, out_specs=out_specs, check_vma=False)
```

```python
import functools
import math

import jax
import jax.numpy as jnp
import numpy as np
from jax import lax
from jax.experimental import pallas as pl
from jax.experimental.pallas import tpu as pltpu
from jax.sharding import PartitionSpec as P

LANES = 128
GROUP = 8
CORES = 2


def dft_tables(length, groups):
    index = np.arange(length)
    phase = (np.outer(index, index) % length) * (2.0 * math.pi / length)
    cosine, sine = np.cos(phase), np.sin(phase)
    table = np.stack([np.stack([cosine, -sine]), np.stack([sine, cosine])])
    table = table.transpose(0, 2, 1, 3).reshape(2 * length, 2, groups, length // groups)
    table = table.transpose(0, 2, 1, 3).reshape(2 * length, 2 * length) / math.sqrt(length)
    high = table.astype(jnp.bfloat16)
    low = (table - high.astype(np.float64)).astype(jnp.bfloat16)
    return high, low


def spectra_kernel(dims, delays_ref, before_ref, own_ref, after_ref, coef_ref, high_ref, low_ref, out_ref, flat, slab, filt):
    tap_count, parts, spectra, hist, skip = dims
    own = own_ref.shape[2]
    groups = out_ref.shape[0]
    frames = spectra + tap_count - 1
    need = -(-frames * parts // GROUP) * GROUP
    step = pl.program_id(0)
    lane = lax.broadcasted_iota(jnp.int32, (need, LANES), 1)
    for c in range(2):
        for j in range(GROUP):
            delay = delays_ref[step * GROUP + j]
            rows, shift = delay // LANES, delay % LANES
            turn = lax.rem(LANES - shift, LANES)
            buf = flat.at[(c * GROUP + j) % flat.shape[0]]
            buf[0:hist, :] = pltpu.roll(before_ref[j, c].astype(jnp.float32), turn, 1)
            buf[hist : hist + own, :] = pltpu.roll(own_ref[j, c].astype(jnp.float32), turn, 1)
            buf[hist + own : hist + own + hist, :] = pltpu.roll(after_ref[j, c].astype(jnp.float32), turn, 1)
            low = buf[pl.ds(rows + skip, need), :]
            high = buf[pl.ds(rows + skip + 1, need), :]
            slab[c, pl.ds(j, need, stride=GROUP), :] = jnp.where(lane < LANES - shift, low, high)
    block = 8
    for c in range(2):
        for h in range(parts):
            for s0 in range(0, spectra, block):
                taps = [coef_ref[m, h] for m in range(tap_count)]
                held = {}
                for s in range(s0, min(s0 + block, spectra)):
                    total = None
                    for m in range(tap_count):
                        row = parts * (s + tap_count - 1 - m) + h
                        if row not in held:
                            held[row] = slab[c, row * GROUP : (row + 1) * GROUP, :]
                        term = taps[m] * held[row]
                        total = term if total is None else total + term
                    filt[s * GROUP : (s + 1) * GROUP, (c * parts + h) * LANES : (c * parts + h + 1) * LANES] = total
    value = filt[...]
    high = value.astype(jnp.bfloat16)
    low = (value - high.astype(jnp.float32)).astype(jnp.bfloat16)
    result = (
        jnp.dot(high, high_ref[...], preferred_element_type=jnp.float32)
        + jnp.dot(low, high_ref[...], preferred_element_type=jnp.float32)
        + jnp.dot(high, low_ref[...], preferred_element_type=jnp.float32)
    )
    width = result.shape[1] // groups
    packs = LANES // width
    rows = spectra * GROUP // packs
    place = lax.broadcasted_iota(jnp.int32, (rows, LANES), 1) // width
    for p in range(groups // packs):
        pieces = [result[j * rows : (j + 1) * rows, p * LANES : (p + 1) * LANES] for j in range(packs)]
        for q in range(packs):
            total = pieces[q]
            for j in range(packs):
                if j != q:
                    moved = pltpu.roll(pieces[j], ((j - q) * width) % LANES, 1)
                    total = jnp.where(place == j, moved, total)
            out_ref[p * packs + q, 0] = total.astype(jnp.bfloat16)


def gram_kernel(scale, which_ref, x_ref, out_ref, mine):
    shards, _, depth, inputs = x_ref.shape
    rows = out_ref.shape[1]
    half = depth // 2
    x = x_ref[...].reshape(shards * depth, inputs)
    for t in range(inputs // rows):

        @pl.when(which_ref[0] == t)
        def _():
            mine[...] = x[:, t * rows : (t + 1) * rows].astype(jnp.float32)

    left = mine[...]
    turned = []
    for t in range(shards):
        turned.append(left[t * depth + half : (t + 1) * depth])
        turned.append(-left[t * depth : t * depth + half])
    turned = jnp.concatenate(turned, axis=0).astype(jnp.bfloat16)
    dims = (((0,), (0,)), ((), ()))
    real = lax.dot_general(left.astype(jnp.bfloat16), x, dims, preferred_element_type=jnp.float32)
    imag = lax.dot_general(turned, x, dims, preferred_element_type=jnp.float32)
    out_ref[0, :, 0:inputs] = real * scale
    out_ref[0, :, inputs : 2 * inputs] = imag * scale


def front(samples, delays, taps):
    tap_count, channels = taps.shape
    local_inputs, _, shard_len = samples.shape
    peers = lax.axis_size("tm")
    groups = lax.axis_size("inp")
    parts = channels // LANES
    spectra = shard_len // channels
    margin_rows = (tap_count - 1) * parts
    hist = -(-margin_rows // 16) * 16
    own = shard_len // LANES
    lined = samples.reshape(local_inputs, 2, own, LANES)
    up = [(i, (i + 1) % peers) for i in range(peers)]
    down = [(j, i) for i, j in up]
    before = lax.ppermute(lined[:, :, own - hist :], "tm", up)
    after = lax.ppermute(lined[:, :, :hist], "tm", down)
    steps = -(-local_inputs // GROUP)
    offsets = jnp.pad(delays, (0, steps * GROUP - local_inputs))
    coef = (taps.astype(jnp.float32) * (1.0 / 4096.0)).reshape(tap_count, parts, 1, LANES)
    coef = jnp.broadcast_to(coef, (tap_count, parts, GROUP, LANES))
    high, low = dft_tables(channels, groups)
    width = 2 * channels // groups
    packs = LANES // width
    rows = spectra * GROUP // packs
    need = -(-(spectra + tap_count - 1) * parts // GROUP) * GROUP
    total = -(-max(2 * hist + own, need + hist + 1) // GROUP) * GROUP
    fixed = lambda shape: pl.BlockSpec(shape, lambda i, d: (0,) * len(shape))
    return pl.pallas_call(
        functools.partial(spectra_kernel, (tap_count, parts, spectra, hist, hist - margin_rows)),
        out_shape=jax.ShapeDtypeStruct((groups, steps, rows, LANES), jnp.bfloat16),
        grid_spec=pltpu.PrefetchScalarGridSpec(
            num_scalar_prefetch=1,
            grid=(steps,),
            in_specs=[
                pl.BlockSpec((GROUP, 2, hist, LANES), lambda i, d: (i, 0, 0, 0)),
                pl.BlockSpec((GROUP, 2, own, LANES), lambda i, d: (i, 0, 0, 0)),
                pl.BlockSpec((GROUP, 2, hist, LANES), lambda i, d: (i, 0, 0, 0)),
                fixed(coef.shape),
                fixed(high.shape),
                fixed(low.shape),
            ],
            out_specs=pl.BlockSpec((groups, 1, rows, LANES), lambda i, d: (0, i, 0, 0)),
            scratch_shapes=[
                pltpu.VMEM((4, total, LANES), jnp.float32),
                pltpu.VMEM((2, need * GROUP, LANES), jnp.float32),
                pltpu.VMEM((spectra * GROUP, 2 * channels), jnp.float32),
            ],
        ),
        name="spectra",
    )(offsets, before, lined, after, coef, jnp.asarray(high), jnp.asarray(low))


def gram(gathered, rows, scale):
    shards, channels, depth, inputs = gathered.shape
    which = lax.axis_index("tm").astype(jnp.int32).reshape(1)
    return pl.pallas_call(
        functools.partial(gram_kernel, scale),
        out_shape=jax.ShapeDtypeStruct((channels, rows, 2 * inputs), jnp.float32),
        grid_spec=pltpu.PrefetchScalarGridSpec(
            num_scalar_prefetch=1,
            grid=(channels,),
            in_specs=[pl.BlockSpec((shards, 1, depth, inputs), lambda f, w: (0, f, 0, 0))],
            out_specs=pl.BlockSpec((1, rows, 2 * inputs), lambda f, w: (f, 0, 0)),
            scratch_shapes=[pltpu.VMEM((shards * depth, rows), jnp.float32)],
        ),
        name="gram",
    )(which, gathered)


def exchange_kernel(sent_ref, out_ref, own_sem, turn_send, turn_recv, far_send, far_recv, near_send, near_recv, pass_send, pass_recv):
    groups, peers = lax.axis_size("inp"), lax.axis_size("tm")
    chips = peers // CORES
    g, t = lax.axis_index("inp"), lax.axis_index("tm")
    y, core = t // CORES, t % CORES
    partner = y * CORES + (CORES - 1 - core)

    def far(step):
        return ((y + step) % chips) * CORES + core

    def back(step):
        return ((y + chips - step) % chips) * CORES + core

    def remote(src, dst, send, recv, to_g, to_t):
        return pltpu.make_async_remote_copy(
            src_ref=src, dst_ref=dst, send_sem=send, recv_sem=recv,
            device_id={"inp": to_g, "tm": to_t}, device_id_type=pl.DeviceIdType.MESH,
        )

    barrier = pltpu.get_barrier_semaphore()
    for o in range(1, groups):
        pl.semaphore_signal(barrier, inc=1, device_id={"inp": (g + o) % groups, "tm": t}, device_id_type=pl.DeviceIdType.MESH)
    for step in range(1, chips):
        pl.semaphore_signal(barrier, inc=1, device_id={"inp": g, "tm": far(step)}, device_id_type=pl.DeviceIdType.MESH)
    pl.semaphore_signal(barrier, inc=1, device_id={"inp": g, "tm": partner}, device_id_type=pl.DeviceIdType.MESH)
    pl.semaphore_wait(barrier, groups - 1 + chips - 1 + 1)

    def turn(o):
        to = (g + o) % groups
        return remote(sent_ref.at[to], out_ref.at[t, g], turn_send.at[o], turn_recv.at[o], to, t)

    def slot(o):
        return out_ref.at[t, (g + groups - o) % groups]

    def spread(o, src):
        dst = slot(o)
        copies = [remote(src, dst, far_send.at[step, o], far_recv.at[step, o], g, far(step)) for step in range(1, chips)]
        return copies + [remote(src, dst, near_send.at[o], near_recv.at[o], g, partner)]

    def relay(step, o):
        piece = out_ref.at[back(step), (g + groups - o) % groups]
        return remote(piece, piece, pass_send.at[step, o], pass_recv.at[step, o], g, partner)

    order = list(range(1, groups))
    for o in order:
        turn(o).start()
    own = pltpu.make_async_copy(sent_ref.at[g], out_ref.at[t, g], own_sem)
    own.start()
    for copy in spread(0, sent_ref.at[g]):
        copy.start()

    def land(o):
        for step in range(1, chips):
            piece = out_ref.at[back(step), (g + groups - o) % groups]
            remote(piece, piece, far_send.at[step, o], far_recv.at[step, o], g, far(step)).wait_recv()
            relay(step, o).start()

    previous = 0
    for o in order:
        turn(o).wait_recv()
        for copy in spread(o, slot(o)):
            copy.start()
        land(previous)
        previous = o
    land(previous)
    own.wait()
    for o in range(groups):
        if o:
            turn(o).wait_send()
        src = slot(o) if o else sent_ref.at[g]
        for copy in spread(o, src):
            copy.wait_send()
        piece = out_ref.at[partner, (g + groups - o) % groups]
        remote(piece, piece, near_send.at[o], near_recv.at[o], g, partner).wait_recv()
        for step in range(1, chips):
            relay(step, o).wait_send()
            other = ((y + chips - step) % chips) * CORES + (CORES - 1 - core)
            piece = out_ref.at[other, (g + groups - o) % groups]
            remote(piece, piece, pass_send.at[step, o], pass_recv.at[step, o], g, partner).wait_recv()


def exchange(sent):
    groups, peers = lax.axis_size("inp"), lax.axis_size("tm")
    chips = peers // CORES
    dma = pltpu.SemaphoreType.DMA
    return pl.pallas_call(
        exchange_kernel,
        out_shape=jax.ShapeDtypeStruct((peers,) + sent.shape, sent.dtype),
        in_specs=[pl.BlockSpec(memory_space=pl.ANY)],
        out_specs=pl.BlockSpec(memory_space=pl.ANY),
        scratch_shapes=[
            dma, dma((groups,)), dma((groups,)), dma((chips, groups)), dma((chips, groups)),
            dma((groups,)), dma((groups,)), dma((chips, groups)), dma((chips, groups)),
        ],
        compiler_params=pltpu.CompilerParams(collective_id=0, has_side_effects=True),
        name="exchange",
    )(sent)


def turned_gram_kernel(scale, channels, which_ref, buf_ref, out_ref, lined, mine):
    peers, groups, steps, rows, _ = buf_ref.shape
    inputs = groups * steps * GROUP
    width = 2 * channels
    packs = LANES // width
    depth = lined.shape[1] // channels
    half = depth // 2
    spectra = half // peers
    per_pack = spectra // packs
    tiles = lined.shape[0]
    height = out_ref.shape[1]
    f = pl.program_id(0)

    @pl.when(f == 0)
    def _():
        @pl.loop(0, peers * (rows // 16))
        def _(index):
            t, pair = index // (rows // 16), index % (rows // 16)
            block = buf_ref[t, :, :, pl.ds(pl.multiple_of(pair * 16, 16), 16), :].astype(jnp.float32)
            block = block.reshape(groups * steps, 2, GROUP, LANES)
            for u in range(2):
                value = block[:, u].reshape(inputs, LANES)
                for a in range(tiles):
                    count = min(LANES, inputs - a * LANES)
                    moved = value[a * LANES : a * LANES + count].T
                    for j in range(packs):
                        for d in range(2):
                            line = d * half + t * spectra + j * per_pack + pair * 2 + u
                            first = j * width + d * channels
                            piece = moved[first : first + channels]
                            if count == LANES:
                                lined[a, pl.ds(line, channels, stride=depth), :] = piece
                            else:
                                lined[a, pl.ds(line, channels, stride=depth), :] = jnp.concatenate(
                                    [piece, jnp.zeros((channels, LANES - count), jnp.float32)], axis=1
                                )

    start = pl.multiple_of(f * depth, 8)
    x = jnp.concatenate([lined[a, pl.ds(start, depth), :] for a in range(tiles)], axis=1)
    for t in range(inputs // height):

        @pl.when(which_ref[0] == t)
        def _():
            mine[...] = x[:, t * height : (t + 1) * height]

    left = mine[...]
    other = jnp.concatenate([left[half:], -left[:half]], axis=0)
    both = jnp.concatenate([left.T, other.T], axis=0).astype(jnp.bfloat16)
    result = jnp.dot(both, x.astype(jnp.bfloat16), preferred_element_type=jnp.float32) * scale
    out_ref[0, :, 0:inputs] = result[:height, :inputs]
    out_ref[0, :, inputs : 2 * inputs] = result[height:, :inputs]


def turned_gram(buf, channels, height, scale):
    peers, groups, steps, rows, _ = buf.shape
    inputs = groups * steps * GROUP
    packs = LANES // (2 * channels)
    depth = 2 * peers * packs * rows // GROUP
    which = lax.axis_index("tm").astype(jnp.int32).reshape(1)
    return pl.pallas_call(
        functools.partial(turned_gram_kernel, scale, channels),
        out_shape=jax.ShapeDtypeStruct((channels, height, 2 * inputs), jnp.float32),
        grid_spec=pltpu.PrefetchScalarGridSpec(
            num_scalar_prefetch=1,
            grid=(channels,),
            in_specs=[pl.BlockSpec(buf.shape, lambda f, w: (0, 0, 0, 0, 0), pipeline_mode=pl.Buffered(1))],
            out_specs=pl.BlockSpec((1, height, 2 * inputs), lambda f, w: (f, 0, 0)),
            scratch_shapes=[
                pltpu.VMEM((-(-inputs // LANES), channels * depth, LANES), jnp.float32),
                pltpu.VMEM((depth, height), jnp.float32),
            ],
        ),
        name="turned_gram",
    )(which, buf)


def shards(samples, delays, taps):
    channels = taps.shape[1]
    local_inputs, _, shard_len = samples.shape
    groups, peers = lax.axis_size("inp"), lax.axis_size("tm")
    inputs = local_inputs * groups
    spectra = shard_len // channels
    mine = channels // groups
    packs = LANES // (2 * mine)
    sent = front(samples, delays, taps)
    if local_inputs % GROUP == 0 and sent.shape[2] % 16 == 0:
        return turned_gram(exchange(sent), mine, inputs // peers, 1.0 / (spectra * peers))
    turned = lax.all_to_all(sent, "inp", split_axis=0, concat_axis=0, tiled=True)
    steps = turned.shape[1]
    turned = turned.reshape(groups, steps, spectra // packs, GROUP, packs, 2, mine)
    turned = turned.transpose(6, 5, 4, 2, 0, 1, 3).reshape(mine, 2 * spectra, groups, steps * GROUP)
    turned = turned[..., :local_inputs].reshape(mine, 2 * spectra, inputs)
    gathered = lax.all_gather(turned, "tm", axis=0, tiled=False)
    return gram(gathered, inputs // peers, 1.0 / (spectra * peers))


def solution(mesh):
    in_specs = (P("inp", None, "tm"), P("inp"), P())
    out_specs = P("inp", "tm", None)
    return jax.shard_map(shards, mesh=mesh, in_specs=in_specs, out_specs=out_specs, check_vma=False)
```

```python
import functools
import math

import jax
import jax.numpy as jnp
import numpy as np
from jax import lax
from jax.experimental import pallas as pl
from jax.experimental.pallas import tpu as pltpu
from jax.sharding import PartitionSpec as P

LANES = 128
GROUP = 8
CORES = 2


def dft_tables(length, groups):
    index = np.arange(length)
    phase = (np.outer(index, index) % length) * (2.0 * math.pi / length)
    cosine, sine = np.cos(phase), np.sin(phase)
    table = np.stack([np.stack([cosine, -sine]), np.stack([sine, cosine])])
    table = table.transpose(0, 2, 1, 3).reshape(2 * length, 2, groups, length // groups)
    table = table.transpose(0, 2, 1, 3).reshape(2 * length, 2 * length) / math.sqrt(length)
    high = table.astype(jnp.bfloat16)
    low = (table - high.astype(np.float64)).astype(jnp.bfloat16)
    return high, low


def spectra_kernel(dims, delays_ref, before_ref, own_ref, after_ref, coef_ref, high_ref, low_ref, out_ref, flat, slab, filt):
    tap_count, parts, spectra, hist, skip = dims
    own = own_ref.shape[2]
    groups = out_ref.shape[0]
    frames = spectra + tap_count - 1
    need = -(-frames * parts // GROUP) * GROUP
    step = pl.program_id(0)
    lane = lax.broadcasted_iota(jnp.int32, (need, LANES), 1)
    for c in range(2):
        for j in range(GROUP):
            delay = delays_ref[step * GROUP + j]
            rows, shift = delay // LANES, delay % LANES
            turn = lax.rem(LANES - shift, LANES)
            buf = flat.at[(c * GROUP + j) % flat.shape[0]]
            buf[0:hist, :] = pltpu.roll(before_ref[j, c].astype(jnp.float32), turn, 1)
            buf[hist : hist + own, :] = pltpu.roll(own_ref[j, c].astype(jnp.float32), turn, 1)
            buf[hist + own : hist + own + hist, :] = pltpu.roll(after_ref[j, c].astype(jnp.float32), turn, 1)
            low = buf[pl.ds(rows + skip, need), :]
            high = buf[pl.ds(rows + skip + 1, need), :]
            slab[c, pl.ds(j, need, stride=GROUP), :] = jnp.where(lane < LANES - shift, low, high)
    block = 8
    for c in range(2):
        for h in range(parts):
            for s0 in range(0, spectra, block):
                taps = [coef_ref[m, h] for m in range(tap_count)]
                held = {}
                for s in range(s0, min(s0 + block, spectra)):
                    total = None
                    for m in range(tap_count):
                        row = parts * (s + tap_count - 1 - m) + h
                        if row not in held:
                            held[row] = slab[c, row * GROUP : (row + 1) * GROUP, :]
                        term = taps[m] * held[row]
                        total = term if total is None else total + term
                    filt[s * GROUP : (s + 1) * GROUP, (c * parts + h) * LANES : (c * parts + h + 1) * LANES] = total
    value = filt[...]
    high = value.astype(jnp.bfloat16)
    low = (value - high.astype(jnp.float32)).astype(jnp.bfloat16)
    result = (
        jnp.dot(high, high_ref[...], preferred_element_type=jnp.float32)
        + jnp.dot(low, high_ref[...], preferred_element_type=jnp.float32)
        + jnp.dot(high, low_ref[...], preferred_element_type=jnp.float32)
    )
    width = result.shape[1] // groups
    packs = LANES // width
    rows = spectra * GROUP // packs
    place = lax.broadcasted_iota(jnp.int32, (rows, LANES), 1) // width
    for p in range(groups // packs):
        pieces = [result[j * rows : (j + 1) * rows, p * LANES : (p + 1) * LANES] for j in range(packs)]
        for q in range(packs):
            total = pieces[q]
            for j in range(packs):
                if j != q:
                    moved = pltpu.roll(pieces[j], ((j - q) * width) % LANES, 1)
                    total = jnp.where(place == j, moved, total)
            out_ref[p * packs + q, 0] = total.astype(jnp.bfloat16)


def gram_kernel(scale, which_ref, x_ref, out_ref, mine):
    shards, _, depth, inputs = x_ref.shape
    rows = out_ref.shape[1]
    half = depth // 2
    x = x_ref[...].reshape(shards * depth, inputs)
    for t in range(inputs // rows):

        @pl.when(which_ref[0] == t)
        def _():
            mine[...] = x[:, t * rows : (t + 1) * rows].astype(jnp.float32)

    left = mine[...]
    turned = []
    for t in range(shards):
        turned.append(left[t * depth + half : (t + 1) * depth])
        turned.append(-left[t * depth : t * depth + half])
    turned = jnp.concatenate(turned, axis=0).astype(jnp.bfloat16)
    dims = (((0,), (0,)), ((), ()))
    real = lax.dot_general(left.astype(jnp.bfloat16), x, dims, preferred_element_type=jnp.float32)
    imag = lax.dot_general(turned, x, dims, preferred_element_type=jnp.float32)
    out_ref[0, :, 0:inputs] = real * scale
    out_ref[0, :, inputs : 2 * inputs] = imag * scale


def front(samples, delays, taps):
    tap_count, channels = taps.shape
    local_inputs, _, shard_len = samples.shape
    peers = lax.axis_size("tm")
    groups = lax.axis_size("inp")
    parts = channels // LANES
    spectra = shard_len // channels
    margin_rows = (tap_count - 1) * parts
    hist = -(-margin_rows // 16) * 16
    own = shard_len // LANES
    lined = samples.reshape(local_inputs, 2, own, LANES)
    up = [(i, (i + 1) % peers) for i in range(peers)]
    down = [(j, i) for i, j in up]
    before = lax.ppermute(lined[:, :, own - hist :], "tm", up)
    after = lax.ppermute(lined[:, :, :hist], "tm", down)
    steps = -(-local_inputs // GROUP)
    offsets = jnp.pad(delays, (0, steps * GROUP - local_inputs))
    coef = (taps.astype(jnp.float32) * (1.0 / 4096.0)).reshape(tap_count, parts, 1, LANES)
    coef = jnp.broadcast_to(coef, (tap_count, parts, GROUP, LANES))
    high, low = dft_tables(channels, groups)
    width = 2 * channels // groups
    packs = LANES // width
    rows = spectra * GROUP // packs
    need = -(-(spectra + tap_count - 1) * parts // GROUP) * GROUP
    total = -(-max(2 * hist + own, need + hist + 1) // GROUP) * GROUP
    fixed = lambda shape: pl.BlockSpec(shape, lambda i, d: (0,) * len(shape))
    return pl.pallas_call(
        functools.partial(spectra_kernel, (tap_count, parts, spectra, hist, hist - margin_rows)),
        out_shape=jax.ShapeDtypeStruct((groups, steps, rows, LANES), jnp.bfloat16),
        grid_spec=pltpu.PrefetchScalarGridSpec(
            num_scalar_prefetch=1,
            grid=(steps,),
            in_specs=[
                pl.BlockSpec((GROUP, 2, hist, LANES), lambda i, d: (i, 0, 0, 0)),
                pl.BlockSpec((GROUP, 2, own, LANES), lambda i, d: (i, 0, 0, 0)),
                pl.BlockSpec((GROUP, 2, hist, LANES), lambda i, d: (i, 0, 0, 0)),
                fixed(coef.shape),
                fixed(high.shape),
                fixed(low.shape),
            ],
            out_specs=pl.BlockSpec((groups, 1, rows, LANES), lambda i, d: (0, i, 0, 0)),
            scratch_shapes=[
                pltpu.VMEM((4, total, LANES), jnp.float32),
                pltpu.VMEM((2, need * GROUP, LANES), jnp.float32),
                pltpu.VMEM((spectra * GROUP, 2 * channels), jnp.float32),
            ],
        ),
        name="spectra",
    )(offsets, before, lined, after, coef, jnp.asarray(high), jnp.asarray(low))


def gram(gathered, rows, scale):
    shards, channels, depth, inputs = gathered.shape
    which = lax.axis_index("tm").astype(jnp.int32).reshape(1)
    return pl.pallas_call(
        functools.partial(gram_kernel, scale),
        out_shape=jax.ShapeDtypeStruct((channels, rows, 2 * inputs), jnp.float32),
        grid_spec=pltpu.PrefetchScalarGridSpec(
            num_scalar_prefetch=1,
            grid=(channels,),
            in_specs=[pl.BlockSpec((shards, 1, depth, inputs), lambda f, w: (0, f, 0, 0))],
            out_specs=pl.BlockSpec((1, rows, 2 * inputs), lambda f, w: (f, 0, 0)),
            scratch_shapes=[pltpu.VMEM((shards * depth, rows), jnp.float32)],
        ),
        name="gram",
    )(which, gathered)


def send_order(groups):
    half = groups // 2
    outer = sorted(range(half, groups), key=lambda o: (-(o // (half // 2 or 1)), o))
    inner = list(range(2, half))
    order = [o for o in (1,) if o < half]
    while outer or inner:
        if outer:
            order.append(outer.pop(0))
        if inner:
            order.append(inner.pop(0))
    return order


def exchange_kernel(sent_ref, out_ref, own_sem, turn_send, turn_recv, far_send, far_recv, near_send, near_recv, pass_send, pass_recv):
    groups, peers = lax.axis_size("inp"), lax.axis_size("tm")
    chips = peers // CORES
    g, t = lax.axis_index("inp"), lax.axis_index("tm")
    y, core = t // CORES, t % CORES
    partner = y * CORES + (CORES - 1 - core)

    def far(step):
        return ((y + step) % chips) * CORES + core

    def back(step):
        return ((y + chips - step) % chips) * CORES + core

    def pair(o):
        bits = [(b, (g // b) % 2) for b in (1 << k for k in range(groups.bit_length() - 1))]
        return sum(b * (1 - bit) if o & b else b * bit for b, bit in bits)

    def remote(src, dst, send, recv, to_g, to_t):
        return pltpu.make_async_remote_copy(
            src_ref=src, dst_ref=dst, send_sem=send, recv_sem=recv,
            device_id={"inp": to_g, "tm": to_t}, device_id_type=pl.DeviceIdType.MESH,
        )

    barrier = pltpu.get_barrier_semaphore()
    for o in range(1, groups):
        pl.semaphore_signal(barrier, inc=1, device_id={"inp": pair(o), "tm": t}, device_id_type=pl.DeviceIdType.MESH)
    for step in range(1, chips):
        pl.semaphore_signal(barrier, inc=1, device_id={"inp": g, "tm": far(step)}, device_id_type=pl.DeviceIdType.MESH)
    pl.semaphore_signal(barrier, inc=1, device_id={"inp": g, "tm": partner}, device_id_type=pl.DeviceIdType.MESH)
    pl.semaphore_wait(barrier, groups - 1 + chips - 1 + 1)

    def turn(o):
        to = pair(o)
        return remote(sent_ref.at[to], out_ref.at[t, g], turn_send.at[o], turn_recv.at[o], to, t)

    def slot(o):
        return out_ref.at[t, pair(o)]

    def spread(o, src):
        dst = slot(o)
        copies = [remote(src, dst, far_send.at[step, o], far_recv.at[step, o], g, far(step)) for step in range(1, chips)]
        return copies + [remote(src, dst, near_send.at[o], near_recv.at[o], g, partner)]

    def relay(step, o):
        piece = out_ref.at[back(step), pair(o)]
        return remote(piece, piece, pass_send.at[step, o], pass_recv.at[step, o], g, partner)

    order = send_order(groups)
    for o in order:
        turn(o).start()
    own = pltpu.make_async_copy(sent_ref.at[g], out_ref.at[t, g], own_sem)
    own.start()
    for copy in spread(0, sent_ref.at[g]):
        copy.start()

    def land(o):
        for step in range(1, chips):
            piece = out_ref.at[back(step), pair(o)]
            remote(piece, piece, far_send.at[step, o], far_recv.at[step, o], g, far(step)).wait_recv()
            relay(step, o).start()

    pending = [0]
    for o in order:
        turn(o).wait_recv()
        for copy in spread(o, slot(o)):
            copy.start()
        pending.append(o)
        if len(pending) > 2:
            land(pending.pop(0))
    for o in pending:
        land(o)
    own.wait()
    for o in range(groups):
        if o:
            turn(o).wait_send()
        src = slot(o) if o else sent_ref.at[g]
        for copy in spread(o, src):
            copy.wait_send()
        piece = out_ref.at[partner, pair(o)]
        remote(piece, piece, near_send.at[o], near_recv.at[o], g, partner).wait_recv()
        for step in range(1, chips):
            relay(step, o).wait_send()
            other = ((y + chips - step) % chips) * CORES + (CORES - 1 - core)
            piece = out_ref.at[other, pair(o)]
            remote(piece, piece, pass_send.at[step, o], pass_recv.at[step, o], g, partner).wait_recv()


def exchange(sent):
    groups, peers = lax.axis_size("inp"), lax.axis_size("tm")
    chips = peers // CORES
    dma = pltpu.SemaphoreType.DMA
    return pl.pallas_call(
        exchange_kernel,
        out_shape=jax.ShapeDtypeStruct((peers,) + sent.shape, sent.dtype),
        in_specs=[pl.BlockSpec(memory_space=pl.ANY)],
        out_specs=pl.BlockSpec(memory_space=pl.ANY),
        scratch_shapes=[
            dma, dma((groups,)), dma((groups,)), dma((chips, groups)), dma((chips, groups)),
            dma((groups,)), dma((groups,)), dma((chips, groups)), dma((chips, groups)),
        ],
        compiler_params=pltpu.CompilerParams(collective_id=0, has_side_effects=True),
        name="exchange",
    )(sent)


def turned_gram_kernel(scale, channels, which_ref, buf_ref, out_ref, lined, mine):
    _, groups, steps, rows, _ = buf_ref.shape
    inputs = groups * steps * GROUP
    width = 2 * channels
    packs = LANES // width
    depth = lined.shape[1] // channels
    half = depth // 2
    per_pack = rows // GROUP
    spectra = per_pack * packs
    peers = half // spectra
    some, height = out_ref.shape[0], out_ref.shape[1]
    taken = height // (steps * GROUP)
    i = pl.program_id(0)

    @pl.when(i < peers)
    def _():
        @pl.loop(0, rows // 16)
        def _(pair):
            span = pl.ds(pl.multiple_of(pair * 16, 16), 16)
            for kept, block in ((lined, buf_ref[0, :, :, span, :]), (mine, buf_ref[0, pl.ds(which_ref[0] * taken, taken), :, span, :])):
                block = block.astype(jnp.float32)
                block = block.reshape(block.shape[0] * steps, 2, GROUP, LANES)
                for u in range(2):
                    value = block[:, u].reshape(block.shape[0] * GROUP, LANES)
                    for a in range(kept.shape[0]):
                        moved = value[a * LANES : (a + 1) * LANES].T
                        count = moved.shape[1]
                        if count < LANES:
                            moved = jnp.concatenate([moved, jnp.zeros((LANES, LANES - count), jnp.float32)], axis=1)
                        for j in range(packs):
                            for d in range(2):
                                line = d * half + i * spectra + j * per_pack + pair * 2 + u
                                first = j * width + d * channels
                                kept[a, pl.ds(line, channels, stride=depth), :] = moved[first : first + channels]

    room = -(-half // LANES) * LANES
    blank = room - half

    def parts(kept, start):
        return [
            jnp.concatenate([kept[a, pl.ds(start + d * half, half), :] for a in range(kept.shape[0])], axis=1)
            for d in range(2)
        ]

    def filled(value):
        if not blank:
            return value
        return jnp.concatenate([value, jnp.zeros((blank, value.shape[1]), value.dtype)], axis=0)

    @pl.when(i >= peers)
    def _():
        for k in range(some):
            start = pl.multiple_of(((i - peers) * some + k) * depth, 8)
            x = jnp.concatenate([filled(v.astype(jnp.bfloat16)) for v in parts(lined, start)], axis=0)
            re, im = [filled(v).T[:height] for v in parts(mine, start)]
            both = jnp.concatenate([jnp.concatenate([re, im], axis=1), jnp.concatenate([im, -re], axis=1)], axis=0)
            result = jnp.dot(both.astype(jnp.bfloat16), x, preferred_element_type=jnp.float32) * scale
            out_ref[k, :, 0:inputs] = result[:height, :inputs]
            out_ref[k, :, inputs : 2 * inputs] = result[height:, :inputs]


def turned_gram(buf, channels, height, scale):
    peers, groups, steps, rows, _ = buf.shape
    inputs = groups * steps * GROUP
    packs = LANES // (2 * channels)
    depth = 2 * peers * packs * rows // GROUP
    some = math.gcd(channels, 4)
    which = lax.axis_index("tm").astype(jnp.int32).reshape(1)
    return pl.pallas_call(
        functools.partial(turned_gram_kernel, scale, channels),
        out_shape=jax.ShapeDtypeStruct((channels, height, 2 * inputs), jnp.float32),
        grid_spec=pltpu.PrefetchScalarGridSpec(
            num_scalar_prefetch=1,
            grid=(peers + channels // some,),
            in_specs=[pl.BlockSpec((1, groups, steps, rows, LANES), lambda i, w: (jnp.minimum(i, peers - 1), 0, 0, 0, 0))],
            out_specs=pl.BlockSpec((some, height, 2 * inputs), lambda i, w: (jnp.maximum(i - peers, 0), 0, 0)),
            scratch_shapes=[
                pltpu.VMEM((-(-inputs // LANES), channels * depth, LANES), jnp.float32),
                pltpu.VMEM((-(-height // LANES), channels * depth, LANES), jnp.float32),
            ],
        ),
        name="turned_gram",
    )(which, buf)


def shards(samples, delays, taps):
    channels = taps.shape[1]
    local_inputs, _, shard_len = samples.shape
    groups, peers = lax.axis_size("inp"), lax.axis_size("tm")
    inputs = local_inputs * groups
    spectra = shard_len // channels
    mine = channels // groups
    packs = LANES // (2 * mine)
    sent = front(samples, delays, taps)
    direct = local_inputs % GROUP == 0 and sent.shape[2] % 16 == 0 and groups & (groups - 1) == 0
    if direct and (inputs // peers) % local_inputs == 0:
        return turned_gram(exchange(sent), mine, inputs // peers, 1.0 / (spectra * peers))
    turned = lax.all_to_all(sent, "inp", split_axis=0, concat_axis=0, tiled=True)
    steps = turned.shape[1]
    turned = turned.reshape(groups, steps, spectra // packs, GROUP, packs, 2, mine)
    turned = turned.transpose(6, 5, 4, 2, 0, 1, 3).reshape(mine, 2 * spectra, groups, steps * GROUP)
    turned = turned[..., :local_inputs].reshape(mine, 2 * spectra, inputs)
    gathered = lax.all_gather(turned, "tm", axis=0, tiled=False)
    return gram(gathered, inputs // peers, 1.0 / (spectra * peers))


def solution(mesh):
    in_specs = (P("inp", None, "tm"), P("inp"), P())
    out_specs = P("inp", "tm", None)
    return jax.shard_map(shards, mesh=mesh, in_specs=in_specs, out_specs=out_specs, check_vma=False)
```

```python
import functools
import math

import jax
import jax.numpy as jnp
import numpy as np
from jax import lax
from jax.experimental import pallas as pl
from jax.experimental.pallas import tpu as pltpu
from jax.sharding import PartitionSpec as P

LANES = 128
GROUP = 8
CORES = 2
CHUNKS = 3


def dft_tables(length, groups):
    index = np.arange(length)
    phase = (np.outer(index, index) % length) * (2.0 * math.pi / length)
    cosine, sine = np.cos(phase), np.sin(phase)
    table = np.stack([np.stack([cosine, -sine]), np.stack([sine, cosine])])
    table = table.transpose(0, 2, 1, 3).reshape(2 * length, 2, groups, length // groups)
    table = table.transpose(0, 2, 1, 3).reshape(2 * length, 2 * length) / math.sqrt(length)
    high = table.astype(jnp.bfloat16)
    low = (table - high.astype(np.float64)).astype(jnp.bfloat16)
    return high, low


def spectra_kernel(dims, delays_ref, before_ref, own_ref, after_ref, coef_ref, high_ref, low_ref, *rest):
    out_ref, flat, slab, filt = rest[-4:]
    tap_count, parts, spectra, hist, skip, base = dims
    own = own_ref.shape[2]
    groups = out_ref.shape[0]
    frames = spectra + tap_count - 1
    need = -(-frames * parts // GROUP) * GROUP
    step = pl.program_id(0) + base
    lane = lax.broadcasted_iota(jnp.int32, (need, LANES), 1)
    for c in range(2):
        for j in range(GROUP):
            delay = delays_ref[step * GROUP + j]
            rows, shift = delay // LANES, delay % LANES
            turn = lax.rem(LANES - shift, LANES)
            buf = flat.at[(c * GROUP + j) % flat.shape[0]]
            buf[0:hist, :] = pltpu.roll(before_ref[j, c].astype(jnp.float32), turn, 1)
            buf[hist : hist + own, :] = pltpu.roll(own_ref[j, c].astype(jnp.float32), turn, 1)
            buf[hist + own : hist + own + hist, :] = pltpu.roll(after_ref[j, c].astype(jnp.float32), turn, 1)
            low = buf[pl.ds(rows + skip, need), :]
            high = buf[pl.ds(rows + skip + 1, need), :]
            slab[c, pl.ds(j, need, stride=GROUP), :] = jnp.where(lane < LANES - shift, low, high)
    block = 8
    for c in range(2):
        for h in range(parts):
            for s0 in range(0, spectra, block):
                taps = [coef_ref[m, h] for m in range(tap_count)]
                held = {}
                for s in range(s0, min(s0 + block, spectra)):
                    total = None
                    for m in range(tap_count):
                        row = parts * (s + tap_count - 1 - m) + h
                        if row not in held:
                            held[row] = slab[c, row * GROUP : (row + 1) * GROUP, :]
                        term = taps[m] * held[row]
                        total = term if total is None else total + term
                    filt[s * GROUP : (s + 1) * GROUP, (c * parts + h) * LANES : (c * parts + h + 1) * LANES] = total
    value = filt[...]
    high = value.astype(jnp.bfloat16)
    low = (value - high.astype(jnp.float32)).astype(jnp.bfloat16)
    result = (
        jnp.dot(high, high_ref[...], preferred_element_type=jnp.float32)
        + jnp.dot(low, high_ref[...], preferred_element_type=jnp.float32)
        + jnp.dot(high, low_ref[...], preferred_element_type=jnp.float32)
    )
    width = result.shape[1] // groups
    packs = LANES // width
    rows = spectra * GROUP // packs
    place = lax.broadcasted_iota(jnp.int32, (rows, LANES), 1) // width
    for p in range(groups // packs):
        pieces = [result[j * rows : (j + 1) * rows, p * LANES : (p + 1) * LANES] for j in range(packs)]
        for q in range(packs):
            total = pieces[q]
            for j in range(packs):
                if j != q:
                    moved = pltpu.roll(pieces[j], ((j - q) * width) % LANES, 1)
                    total = jnp.where(place == j, moved, total)
            out_ref[p * packs + q, 0] = total.astype(jnp.bfloat16)


def gram_kernel(scale, which_ref, x_ref, out_ref, mine):
    shards, _, depth, inputs = x_ref.shape
    rows = out_ref.shape[1]
    half = depth // 2
    x = x_ref[...].reshape(shards * depth, inputs)
    for t in range(inputs // rows):

        @pl.when(which_ref[0] == t)
        def _():
            mine[...] = x[:, t * rows : (t + 1) * rows].astype(jnp.float32)

    left = mine[...]
    turned = []
    for t in range(shards):
        turned.append(left[t * depth + half : (t + 1) * depth])
        turned.append(-left[t * depth : t * depth + half])
    turned = jnp.concatenate(turned, axis=0).astype(jnp.bfloat16)
    dims = (((0,), (0,)), ((), ()))
    real = lax.dot_general(left.astype(jnp.bfloat16), x, dims, preferred_element_type=jnp.float32)
    imag = lax.dot_general(turned, x, dims, preferred_element_type=jnp.float32)
    out_ref[0, :, 0:inputs] = real * scale
    out_ref[0, :, inputs : 2 * inputs] = imag * scale


def front(samples, delays, taps):
    tap_count, channels = taps.shape
    local_inputs, _, shard_len = samples.shape
    peers = lax.axis_size("tm")
    groups = lax.axis_size("inp")
    parts = channels // LANES
    spectra = shard_len // channels
    margin_rows = (tap_count - 1) * parts
    hist = -(-margin_rows // 16) * 16
    own = shard_len // LANES
    up = [(i, (i + 1) % peers) for i in range(peers)]
    down = [(j, i) for i, j in up]
    steps = -(-local_inputs // GROUP)
    chunks = CHUNKS if local_inputs % (GROUP * CHUNKS) == 0 else 1
    span = local_inputs // chunks
    halos = []
    for k in range(chunks):
        piece = samples[k * span : (k + 1) * span]
        tail = piece[:, :, shard_len - hist * LANES :].reshape(span, 2, hist, LANES)
        head = piece[:, :, : hist * LANES].reshape(span, 2, hist, LANES)
        halos.append((lax.ppermute(tail, "tm", up), lax.ppermute(head, "tm", down)))
    lined = samples.reshape(local_inputs, 2, own, LANES)
    offsets = jnp.pad(delays, (0, steps * GROUP - local_inputs))
    coef = (taps.astype(jnp.float32) * (1.0 / 4096.0)).reshape(tap_count, parts, 1, LANES)
    coef = jnp.broadcast_to(coef, (tap_count, parts, GROUP, LANES))
    high, low = dft_tables(channels, groups)
    width = 2 * channels // groups
    packs = LANES // width
    rows = spectra * GROUP // packs
    need = -(-(spectra + tap_count - 1) * parts // GROUP) * GROUP
    total = -(-max(2 * hist + own, need + hist + 1) // GROUP) * GROUP
    fixed = lambda shape: pl.BlockSpec(shape, lambda i, d: (0,) * len(shape))
    sent = None
    for k in range(chunks):
        base, count = k * steps // chunks, steps // chunks
        before, after = halos[k]
        operands = [offsets, before, lined, after, coef, jnp.asarray(high), jnp.asarray(low)]
        in_specs = [
            pl.BlockSpec((GROUP, 2, hist, LANES), lambda i, d: (i, 0, 0, 0)),
            pl.BlockSpec((GROUP, 2, own, LANES), lambda i, d, base=base: (i + base, 0, 0, 0)),
            pl.BlockSpec((GROUP, 2, hist, LANES), lambda i, d: (i, 0, 0, 0)),
            fixed(coef.shape),
            fixed(high.shape),
            fixed(low.shape),
        ]
        aliases = {}
        if sent is not None:
            aliases = {len(operands): 0}
            operands.append(sent)
            in_specs.append(pl.BlockSpec(memory_space=pl.ANY))
        flops = 6 * count * GROUP * spectra * (2 * channels) ** 2
        sent = pl.pallas_call(
            functools.partial(spectra_kernel, (tap_count, parts, spectra, hist, hist - margin_rows, base)),
            out_shape=jax.ShapeDtypeStruct((groups, steps, rows, LANES), jnp.bfloat16),
            grid_spec=pltpu.PrefetchScalarGridSpec(
                num_scalar_prefetch=1,
                grid=(count,),
                in_specs=in_specs,
                out_specs=pl.BlockSpec((groups, 1, rows, LANES), lambda i, d, base=base: (0, i + base, 0, 0)),
                scratch_shapes=[
                    pltpu.VMEM((4, total, LANES), jnp.float32),
                    pltpu.VMEM((2, need * GROUP, LANES), jnp.float32),
                    pltpu.VMEM((spectra * GROUP, 2 * channels), jnp.float32),
                ],
            ),
            input_output_aliases=aliases,
            cost_estimate=pl.CostEstimate(flops=flops, bytes_accessed=16 << 20, transcendentals=0),
            name="spectra",
        )(*operands)
    return sent


def gram(gathered, rows, scale):
    shards, channels, depth, inputs = gathered.shape
    which = lax.axis_index("tm").astype(jnp.int32).reshape(1)
    return pl.pallas_call(
        functools.partial(gram_kernel, scale),
        out_shape=jax.ShapeDtypeStruct((channels, rows, 2 * inputs), jnp.float32),
        grid_spec=pltpu.PrefetchScalarGridSpec(
            num_scalar_prefetch=1,
            grid=(channels,),
            in_specs=[pl.BlockSpec((shards, 1, depth, inputs), lambda f, w: (0, f, 0, 0))],
            out_specs=pl.BlockSpec((1, rows, 2 * inputs), lambda f, w: (f, 0, 0)),
            scratch_shapes=[pltpu.VMEM((shards * depth, rows), jnp.float32)],
        ),
        name="gram",
    )(which, gathered)


def send_order(groups):
    half = groups // 2
    outer = sorted(range(half, groups), key=lambda o: (-(o // (half // 2 or 1)), o))
    inner = list(range(2, half))
    order = [o for o in (1,) if o < half]
    while outer or inner:
        if outer:
            order.append(outer.pop(0))
        if inner:
            order.append(inner.pop(0))
    return order


def exchange_kernel(sent_ref, out_ref, own_sem, turn_send, turn_recv, far_send, far_recv, near_send, near_recv, pass_send, pass_recv):
    groups, peers = lax.axis_size("inp"), lax.axis_size("tm")
    chips = peers // CORES
    g, t = lax.axis_index("inp"), lax.axis_index("tm")
    y, core = t // CORES, t % CORES
    partner = y * CORES + (CORES - 1 - core)

    def far(step):
        return ((y + step) % chips) * CORES + core

    def back(step):
        return ((y + chips - step) % chips) * CORES + core

    def pair(o):
        bits = [(b, (g // b) % 2) for b in (1 << k for k in range(groups.bit_length() - 1))]
        return sum(b * (1 - bit) if o & b else b * bit for b, bit in bits)

    def remote(src, dst, send, recv, to_g, to_t):
        return pltpu.make_async_remote_copy(
            src_ref=src, dst_ref=dst, send_sem=send, recv_sem=recv,
            device_id={"inp": to_g, "tm": to_t}, device_id_type=pl.DeviceIdType.MESH,
        )

    barrier = pltpu.get_barrier_semaphore()
    for o in range(1, groups):
        pl.semaphore_signal(barrier, inc=1, device_id={"inp": pair(o), "tm": t}, device_id_type=pl.DeviceIdType.MESH)
    for step in range(1, chips):
        pl.semaphore_signal(barrier, inc=1, device_id={"inp": g, "tm": far(step)}, device_id_type=pl.DeviceIdType.MESH)
    pl.semaphore_signal(barrier, inc=1, device_id={"inp": g, "tm": partner}, device_id_type=pl.DeviceIdType.MESH)
    pl.semaphore_wait(barrier, groups - 1 + chips - 1 + 1)

    def turn(o):
        to = pair(o)
        return remote(sent_ref.at[to], out_ref.at[t, g], turn_send.at[o], turn_recv.at[o], to, t)

    def slot(o):
        return out_ref.at[t, pair(o)]

    def spread(o, src):
        dst = slot(o)
        copies = [remote(src, dst, far_send.at[step, o], far_recv.at[step, o], g, far(step)) for step in range(1, chips)]
        return copies + [remote(src, dst, near_send.at[o], near_recv.at[o], g, partner)]

    def relay(step, o):
        piece = out_ref.at[back(step), pair(o)]
        return remote(piece, piece, pass_send.at[step, o], pass_recv.at[step, o], g, partner)

    order = send_order(groups)
    for o in order:
        turn(o).start()
    own = pltpu.make_async_copy(sent_ref.at[g], out_ref.at[t, g], own_sem)
    own.start()
    for copy in spread(0, sent_ref.at[g]):
        copy.start()

    def land(o):
        for step in range(1, chips):
            piece = out_ref.at[back(step), pair(o)]
            remote(piece, piece, far_send.at[step, o], far_recv.at[step, o], g, far(step)).wait_recv()
            relay(step, o).start()

    pending = [0]
    for o in order:
        turn(o).wait_recv()
        for copy in spread(o, slot(o)):
            copy.start()
        pending.append(o)
        if len(pending) > 2:
            land(pending.pop(0))
    for o in pending:
        land(o)
    own.wait()
    for o in range(groups):
        if o:
            turn(o).wait_send()
        src = slot(o) if o else sent_ref.at[g]
        for copy in spread(o, src):
            copy.wait_send()
        piece = out_ref.at[partner, pair(o)]
        remote(piece, piece, near_send.at[o], near_recv.at[o], g, partner).wait_recv()
        for step in range(1, chips):
            relay(step, o).wait_send()
            other = ((y + chips - step) % chips) * CORES + (CORES - 1 - core)
            piece = out_ref.at[other, pair(o)]
            remote(piece, piece, pass_send.at[step, o], pass_recv.at[step, o], g, partner).wait_recv()


def exchange(sent):
    groups, peers = lax.axis_size("inp"), lax.axis_size("tm")
    chips = peers // CORES
    dma = pltpu.SemaphoreType.DMA
    return pl.pallas_call(
        exchange_kernel,
        out_shape=jax.ShapeDtypeStruct((peers,) + sent.shape, sent.dtype),
        in_specs=[pl.BlockSpec(memory_space=pl.ANY)],
        out_specs=pl.BlockSpec(memory_space=pl.ANY),
        scratch_shapes=[
            dma, dma((groups,)), dma((groups,)), dma((chips, groups)), dma((chips, groups)),
            dma((groups,)), dma((groups,)), dma((chips, groups)), dma((chips, groups)),
        ],
        compiler_params=pltpu.CompilerParams(collective_id=0, has_side_effects=True),
        name="exchange",
    )(sent)


def turned_gram_kernel(scale, channels, which_ref, buf_ref, out_ref, lined, mine):
    _, groups, steps, rows, _ = buf_ref.shape
    inputs = groups * steps * GROUP
    width = 2 * channels
    packs = LANES // width
    depth = lined.shape[1] // channels
    half = depth // 2
    per_pack = rows // GROUP
    spectra = per_pack * packs
    peers = half // spectra
    some, height = out_ref.shape[0], out_ref.shape[1]
    taken = height // (steps * GROUP)
    i = pl.program_id(0)

    @pl.when(i < peers)
    def _():
        @pl.loop(0, rows // 16)
        def _(pair):
            span = pl.ds(pl.multiple_of(pair * 16, 16), 16)
            for kept, block in ((lined, buf_ref[0, :, :, span, :]), (mine, buf_ref[0, pl.ds(which_ref[0] * taken, taken), :, span, :])):
                block = block.astype(jnp.float32)
                block = block.reshape(block.shape[0] * steps, 2, GROUP, LANES)
                for u in range(2):
                    value = block[:, u].reshape(block.shape[0] * GROUP, LANES)
                    for a in range(kept.shape[0]):
                        moved = value[a * LANES : (a + 1) * LANES].T
                        count = moved.shape[1]
                        if count < LANES:
                            moved = jnp.concatenate([moved, jnp.zeros((LANES, LANES - count), jnp.float32)], axis=1)
                        for j in range(packs):
                            for d in range(2):
                                line = d * half + i * spectra + j * per_pack + pair * 2 + u
                                first = j * width + d * channels
                                kept[a, pl.ds(line, channels, stride=depth), :] = moved[first : first + channels]

    room = -(-half // LANES) * LANES
    blank = room - half

    def parts(kept, start):
        return [
            jnp.concatenate([kept[a, pl.ds(start + d * half, half), :] for a in range(kept.shape[0])], axis=1)
            for d in range(2)
        ]

    def filled(value):
        if not blank:
            return value
        return jnp.concatenate([value, jnp.zeros((blank, value.shape[1]), value.dtype)], axis=0)

    @pl.when(i >= peers)
    def _():
        for k in range(some):
            start = pl.multiple_of(((i - peers) * some + k) * depth, 8)
            x = jnp.concatenate([filled(v.astype(jnp.bfloat16)) for v in parts(lined, start)], axis=0)
            re, im = [filled(v).T[:height] for v in parts(mine, start)]
            both = jnp.concatenate([jnp.concatenate([re, im], axis=1), jnp.concatenate([im, -re], axis=1)], axis=0)
            result = jnp.dot(both.astype(jnp.bfloat16), x, preferred_element_type=jnp.float32) * scale
            out_ref[k, :, 0:inputs] = result[:height, :inputs]
            out_ref[k, :, inputs : 2 * inputs] = result[height:, :inputs]


def turned_gram(buf, channels, height, scale):
    peers, groups, steps, rows, _ = buf.shape
    inputs = groups * steps * GROUP
    packs = LANES // (2 * channels)
    depth = 2 * peers * packs * rows // GROUP
    some = math.gcd(channels, 4)
    which = lax.axis_index("tm").astype(jnp.int32).reshape(1)
    return pl.pallas_call(
        functools.partial(turned_gram_kernel, scale, channels),
        out_shape=jax.ShapeDtypeStruct((channels, height, 2 * inputs), jnp.float32),
        grid_spec=pltpu.PrefetchScalarGridSpec(
            num_scalar_prefetch=1,
            grid=(peers + channels // some,),
            in_specs=[pl.BlockSpec((1, groups, steps, rows, LANES), lambda i, w: (jnp.minimum(i, peers - 1), 0, 0, 0, 0))],
            out_specs=pl.BlockSpec((some, height, 2 * inputs), lambda i, w: (jnp.maximum(i - peers, 0), 0, 0)),
            scratch_shapes=[
                pltpu.VMEM((-(-inputs // LANES), channels * depth, LANES), jnp.float32),
                pltpu.VMEM((-(-height // LANES), channels * depth, LANES), jnp.float32),
            ],
        ),
        name="turned_gram",
    )(which, buf)


def shards(samples, delays, taps):
    channels = taps.shape[1]
    local_inputs, _, shard_len = samples.shape
    groups, peers = lax.axis_size("inp"), lax.axis_size("tm")
    inputs = local_inputs * groups
    spectra = shard_len // channels
    mine = channels // groups
    packs = LANES // (2 * mine)
    sent = front(samples, delays, taps)
    direct = local_inputs % GROUP == 0 and sent.shape[2] % 16 == 0 and groups & (groups - 1) == 0
    if direct and (inputs // peers) % local_inputs == 0:
        return turned_gram(exchange(sent), mine, inputs // peers, 1.0 / (spectra * peers))
    turned = lax.all_to_all(sent, "inp", split_axis=0, concat_axis=0, tiled=True)
    steps = turned.shape[1]
    turned = turned.reshape(groups, steps, spectra // packs, GROUP, packs, 2, mine)
    turned = turned.transpose(6, 5, 4, 2, 0, 1, 3).reshape(mine, 2 * spectra, groups, steps * GROUP)
    turned = turned[..., :local_inputs].reshape(mine, 2 * spectra, inputs)
    gathered = lax.all_gather(turned, "tm", axis=0, tiled=False)
    return gram(gathered, inputs // peers, 1.0 / (spectra * peers))


def solution(mesh):
    in_specs = (P("inp", None, "tm"), P("inp"), P())
    out_specs = P("inp", "tm", None)
    return jax.shard_map(shards, mesh=mesh, in_specs=in_specs, out_specs=out_specs, check_vma=False)
```

```python
import functools
import math

import jax
import jax.numpy as jnp
import numpy as np
from jax import lax
from jax.experimental import pallas as pl
from jax.experimental.pallas import tpu as pltpu
from jax.sharding import PartitionSpec as P

LANES = 128
GROUP = 8
CORES = 2
CHUNKS = 3


def dft_tables(length, groups):
    index = np.arange(length)
    phase = (np.outer(index, index) % length) * (2.0 * math.pi / length)
    cosine, sine = np.cos(phase), np.sin(phase)
    table = np.stack([np.stack([cosine, -sine]), np.stack([sine, cosine])])
    table = table.transpose(0, 2, 1, 3).reshape(2 * length, 2, groups, length // groups)
    table = table.transpose(0, 2, 1, 3).reshape(2 * length, 2 * length) / math.sqrt(length)
    high = table.astype(jnp.bfloat16)
    low = (table - high.astype(np.float64)).astype(jnp.bfloat16)
    return high, low


def spectra_kernel(dims, delays_ref, before_ref, own_ref, after_ref, coef_ref, high_ref, low_ref, *rest):
    out_ref, flat, slab, filt = rest[-4:]
    tap_count, parts, spectra, hist, skip, base = dims
    own = own_ref.shape[2]
    groups = out_ref.shape[0]
    frames = spectra + tap_count - 1
    need = -(-frames * parts // GROUP) * GROUP
    step = pl.program_id(0) + base
    lane = lax.broadcasted_iota(jnp.int32, (need, LANES), 1)
    for c in range(2):
        for j in range(GROUP):
            delay = delays_ref[step * GROUP + j]
            rows, shift = delay // LANES, delay % LANES
            turn = lax.rem(LANES - shift, LANES)
            buf = flat.at[(c * GROUP + j) % flat.shape[0]]
            buf[0:hist, :] = pltpu.roll(before_ref[j, c].astype(jnp.float32), turn, 1)
            buf[hist : hist + own, :] = pltpu.roll(own_ref[j, c].astype(jnp.float32), turn, 1)
            buf[hist + own : hist + own + hist, :] = pltpu.roll(after_ref[j, c].astype(jnp.float32), turn, 1)
            low = buf[pl.ds(rows + skip, need), :]
            high = buf[pl.ds(rows + skip + 1, need), :]
            slab[c, pl.ds(j, need, stride=GROUP), :] = jnp.where(lane < LANES - shift, low, high)
    block = 8
    for c in range(2):
        for h in range(parts):
            for s0 in range(0, spectra, block):
                taps = [coef_ref[m, h] for m in range(tap_count)]
                held = {}
                for s in range(s0, min(s0 + block, spectra)):
                    total = None
                    for m in range(tap_count):
                        row = parts * (s + tap_count - 1 - m) + h
                        if row not in held:
                            held[row] = slab[c, row * GROUP : (row + 1) * GROUP, :]
                        term = taps[m] * held[row]
                        total = term if total is None else total + term
                    filt[s * GROUP : (s + 1) * GROUP, (c * parts + h) * LANES : (c * parts + h + 1) * LANES] = total
    value = filt[...]
    high = value.astype(jnp.bfloat16)
    low = (value - high.astype(jnp.float32)).astype(jnp.bfloat16)
    result = (
        jnp.dot(high, high_ref[...], preferred_element_type=jnp.float32)
        + jnp.dot(low, high_ref[...], preferred_element_type=jnp.float32)
        + jnp.dot(high, low_ref[...], preferred_element_type=jnp.float32)
    )
    width = result.shape[1] // groups
    packs = LANES // width
    rows = spectra * GROUP // packs
    place = lax.broadcasted_iota(jnp.int32, (rows, LANES), 1) // width
    for p in range(groups // packs):
        pieces = [result[j * rows : (j + 1) * rows, p * LANES : (p + 1) * LANES] for j in range(packs)]
        for q in range(packs):
            total = pieces[q]
            for j in range(packs):
                if j != q:
                    moved = pltpu.roll(pieces[j], ((j - q) * width) % LANES, 1)
                    total = jnp.where(place == j, moved, total)
            out_ref[p * packs + q, 0] = total.astype(jnp.bfloat16)


def gram_kernel(scale, which_ref, x_ref, out_ref, mine):
    shards, _, depth, inputs = x_ref.shape
    rows = out_ref.shape[1]
    half = depth // 2
    x = x_ref[...].reshape(shards * depth, inputs)
    for t in range(inputs // rows):

        @pl.when(which_ref[0] == t)
        def _():
            mine[...] = x[:, t * rows : (t + 1) * rows].astype(jnp.float32)

    left = mine[...]
    turned = []
    for t in range(shards):
        turned.append(left[t * depth + half : (t + 1) * depth])
        turned.append(-left[t * depth : t * depth + half])
    turned = jnp.concatenate(turned, axis=0).astype(jnp.bfloat16)
    dims = (((0,), (0,)), ((), ()))
    real = lax.dot_general(left.astype(jnp.bfloat16), x, dims, preferred_element_type=jnp.float32)
    imag = lax.dot_general(turned, x, dims, preferred_element_type=jnp.float32)
    out_ref[0, :, 0:inputs] = real * scale
    out_ref[0, :, inputs : 2 * inputs] = imag * scale


def front(samples, delays, taps):
    tap_count, channels = taps.shape
    local_inputs, _, shard_len = samples.shape
    peers = lax.axis_size("tm")
    groups = lax.axis_size("inp")
    parts = channels // LANES
    spectra = shard_len // channels
    margin_rows = (tap_count - 1) * parts
    hist = -(-margin_rows // 16) * 16
    own = shard_len // LANES
    up = [(i, (i + 1) % peers) for i in range(peers)]
    down = [(j, i) for i, j in up]
    steps = -(-local_inputs // GROUP)
    chunks = CHUNKS if local_inputs % (GROUP * CHUNKS) == 0 else 1
    span = local_inputs // chunks
    lined = samples.reshape(local_inputs, 2, own, LANES)
    halos = []
    for k in range(chunks):
        piece = lined[k * span : (k + 1) * span]
        tail, head = piece[:, :, own - hist :], piece[:, :, :hist]
        halos.append((lax.ppermute(tail, "tm", up), lax.ppermute(head, "tm", down)))
    offsets = jnp.pad(delays, (0, steps * GROUP - local_inputs))
    coef = (taps.astype(jnp.float32) * (1.0 / 4096.0)).reshape(tap_count, parts, 1, LANES)
    coef = jnp.broadcast_to(coef, (tap_count, parts, GROUP, LANES))
    high, low = dft_tables(channels, groups)
    width = 2 * channels // groups
    packs = LANES // width
    rows = spectra * GROUP // packs
    need = -(-(spectra + tap_count - 1) * parts // GROUP) * GROUP
    total = -(-max(2 * hist + own, need + hist + 1) // GROUP) * GROUP
    fixed = lambda shape: pl.BlockSpec(shape, lambda i, d: (0,) * len(shape))
    sent = None
    for k in range(chunks):
        base, count = k * steps // chunks, steps // chunks
        before, after = halos[k]
        operands = [offsets, before, lined, after, coef, jnp.asarray(high), jnp.asarray(low)]
        in_specs = [
            pl.BlockSpec((GROUP, 2, hist, LANES), lambda i, d: (i, 0, 0, 0)),
            pl.BlockSpec((GROUP, 2, own, LANES), lambda i, d, base=base: (i + base, 0, 0, 0)),
            pl.BlockSpec((GROUP, 2, hist, LANES), lambda i, d: (i, 0, 0, 0)),
            fixed(coef.shape),
            fixed(high.shape),
            fixed(low.shape),
        ]
        aliases = {}
        if sent is not None:
            aliases = {len(operands): 0}
            operands.append(sent)
            in_specs.append(pl.BlockSpec(memory_space=pl.ANY))
        flops = 6 * count * GROUP * spectra * (2 * channels) ** 2
        sent = pl.pallas_call(
            functools.partial(spectra_kernel, (tap_count, parts, spectra, hist, hist - margin_rows, base)),
            out_shape=jax.ShapeDtypeStruct((groups, steps, rows, LANES), jnp.bfloat16),
            grid_spec=pltpu.PrefetchScalarGridSpec(
                num_scalar_prefetch=1,
                grid=(count,),
                in_specs=in_specs,
                out_specs=pl.BlockSpec((groups, 1, rows, LANES), lambda i, d, base=base: (0, i + base, 0, 0)),
                scratch_shapes=[
                    pltpu.VMEM((4, total, LANES), jnp.float32),
                    pltpu.VMEM((2, need * GROUP, LANES), jnp.float32),
                    pltpu.VMEM((spectra * GROUP, 2 * channels), jnp.float32),
                ],
            ),
            input_output_aliases=aliases,
            cost_estimate=pl.CostEstimate(flops=flops, bytes_accessed=16 << 20, transcendentals=0),
            name="spectra",
        )(*operands)
    return sent


def gram(gathered, rows, scale):
    shards, channels, depth, inputs = gathered.shape
    which = lax.axis_index("tm").astype(jnp.int32).reshape(1)
    return pl.pallas_call(
        functools.partial(gram_kernel, scale),
        out_shape=jax.ShapeDtypeStruct((channels, rows, 2 * inputs), jnp.float32),
        grid_spec=pltpu.PrefetchScalarGridSpec(
            num_scalar_prefetch=1,
            grid=(channels,),
            in_specs=[pl.BlockSpec((shards, 1, depth, inputs), lambda f, w: (0, f, 0, 0))],
            out_specs=pl.BlockSpec((1, rows, 2 * inputs), lambda f, w: (f, 0, 0)),
            scratch_shapes=[pltpu.VMEM((shards * depth, rows), jnp.float32)],
        ),
        name="gram",
    )(which, gathered)


def send_order(groups):
    half = groups // 2
    outer = sorted(range(half, groups), key=lambda o: (-(o // (half // 2 or 1)), o))
    inner = list(range(2, half))
    order = [o for o in (1,) if o < half]
    while outer or inner:
        if outer:
            order.append(outer.pop(0))
        if inner:
            order.append(inner.pop(0))
    return order


def exchange_kernel(sent_ref, out_ref, own_sem, turn_send, turn_recv, far_send, far_recv, near_send, near_recv, pass_send, pass_recv):
    groups, peers = lax.axis_size("inp"), lax.axis_size("tm")
    chips = peers // CORES
    g, t = lax.axis_index("inp"), lax.axis_index("tm")
    y, core = t // CORES, t % CORES
    partner = y * CORES + (CORES - 1 - core)

    def far(step):
        return ((y + step) % chips) * CORES + core

    def back(step):
        return ((y + chips - step) % chips) * CORES + core

    def pair(o):
        bits = [(b, (g // b) % 2) for b in (1 << k for k in range(groups.bit_length() - 1))]
        return sum(b * (1 - bit) if o & b else b * bit for b, bit in bits)

    def remote(src, dst, send, recv, to_g, to_t):
        return pltpu.make_async_remote_copy(
            src_ref=src, dst_ref=dst, send_sem=send, recv_sem=recv,
            device_id={"inp": to_g, "tm": to_t}, device_id_type=pl.DeviceIdType.MESH,
        )

    barrier = pltpu.get_barrier_semaphore()
    for o in range(1, groups):
        pl.semaphore_signal(barrier, inc=1, device_id={"inp": pair(o), "tm": t}, device_id_type=pl.DeviceIdType.MESH)
    for step in range(1, chips):
        pl.semaphore_signal(barrier, inc=1, device_id={"inp": g, "tm": far(step)}, device_id_type=pl.DeviceIdType.MESH)
    pl.semaphore_signal(barrier, inc=1, device_id={"inp": g, "tm": partner}, device_id_type=pl.DeviceIdType.MESH)
    pl.semaphore_wait(barrier, groups - 1 + chips - 1 + 1)

    def turn(o):
        to = pair(o)
        return remote(sent_ref.at[to], out_ref.at[t, g], turn_send.at[o], turn_recv.at[o], to, t)

    def slot(o):
        return out_ref.at[t, pair(o)]

    def spread(o, src):
        dst = slot(o)
        copies = [remote(src, dst, far_send.at[step, o], far_recv.at[step, o], g, far(step)) for step in range(1, chips)]
        return copies + [remote(src, dst, near_send.at[o], near_recv.at[o], g, partner)]

    def relay(step, o):
        piece = out_ref.at[back(step), pair(o)]
        return remote(piece, piece, pass_send.at[step, o], pass_recv.at[step, o], g, partner)

    order = send_order(groups)
    for o in order:
        turn(o).start()
    own = pltpu.make_async_copy(sent_ref.at[g], out_ref.at[t, g], own_sem)
    own.start()
    for copy in spread(0, sent_ref.at[g]):
        copy.start()

    def land(o):
        for step in range(1, chips):
            piece = out_ref.at[back(step), pair(o)]
            remote(piece, piece, far_send.at[step, o], far_recv.at[step, o], g, far(step)).wait_recv()
            relay(step, o).start()

    pending = [0]
    for o in order:
        turn(o).wait_recv()
        for copy in spread(o, slot(o)):
            copy.start()
        pending.append(o)
        if len(pending) > 2:
            land(pending.pop(0))
    for o in pending:
        land(o)
    own.wait()
    for o in range(groups):
        if o:
            turn(o).wait_send()
        src = slot(o) if o else sent_ref.at[g]
        for copy in spread(o, src):
            copy.wait_send()
        piece = out_ref.at[partner, pair(o)]
        remote(piece, piece, near_send.at[o], near_recv.at[o], g, partner).wait_recv()
        for step in range(1, chips):
            relay(step, o).wait_send()
            other = ((y + chips - step) % chips) * CORES + (CORES - 1 - core)
            piece = out_ref.at[other, pair(o)]
            remote(piece, piece, pass_send.at[step, o], pass_recv.at[step, o], g, partner).wait_recv()


def exchange(sent):
    groups, peers = lax.axis_size("inp"), lax.axis_size("tm")
    chips = peers // CORES
    dma = pltpu.SemaphoreType.DMA
    return pl.pallas_call(
        exchange_kernel,
        out_shape=jax.ShapeDtypeStruct((peers,) + sent.shape, sent.dtype),
        in_specs=[pl.BlockSpec(memory_space=pl.ANY)],
        out_specs=pl.BlockSpec(memory_space=pl.ANY),
        scratch_shapes=[
            dma, dma((groups,)), dma((groups,)), dma((chips, groups)), dma((chips, groups)),
            dma((groups,)), dma((groups,)), dma((chips, groups)), dma((chips, groups)),
        ],
        compiler_params=pltpu.CompilerParams(collective_id=0, has_side_effects=True),
        name="exchange",
    )(sent)


def turned_gram_kernel(scale, channels, which_ref, buf_ref, out_ref, lined, mine):
    _, groups, steps, rows, _ = buf_ref.shape
    inputs = groups * steps * GROUP
    width = 2 * channels
    packs = LANES // width
    depth = lined.shape[1] // channels
    half = depth // 2
    per_pack = rows // GROUP
    spectra = per_pack * packs
    peers = half // spectra
    some, height = out_ref.shape[0], out_ref.shape[1]
    taken = height // (steps * GROUP)
    i = pl.program_id(0)

    @pl.when(i < peers)
    def _():
        @pl.loop(0, rows // 16)
        def _(pair):
            span = pl.ds(pl.multiple_of(pair * 16, 16), 16)
            for kept, block in ((lined, buf_ref[0, :, :, span, :]), (mine, buf_ref[0, pl.ds(which_ref[0] * taken, taken), :, span, :])):
                block = block.astype(jnp.float32)
                block = block.reshape(block.shape[0] * steps, 2, GROUP, LANES)
                for u in range(2):
                    value = block[:, u].reshape(block.shape[0] * GROUP, LANES)
                    for a in range(kept.shape[0]):
                        moved = value[a * LANES : (a + 1) * LANES].T
                        count = moved.shape[1]
                        if count < LANES:
                            moved = jnp.concatenate([moved, jnp.zeros((LANES, LANES - count), jnp.float32)], axis=1)
                        for j in range(packs):
                            for d in range(2):
                                line = d * half + i * spectra + j * per_pack + pair * 2 + u
                                first = j * width + d * channels
                                kept[a, pl.ds(line, channels, stride=depth), :] = moved[first : first + channels]

    room = -(-half // LANES) * LANES
    blank = room - half

    def parts(kept, start):
        return [
            jnp.concatenate([kept[a, pl.ds(start + d * half, half), :] for a in range(kept.shape[0])], axis=1)
            for d in range(2)
        ]

    def filled(value):
        if not blank:
            return value
        return jnp.concatenate([value, jnp.zeros((blank, value.shape[1]), value.dtype)], axis=0)

    @pl.when(i >= peers)
    def _():
        for k in range(some):
            start = pl.multiple_of(((i - peers) * some + k) * depth, 8)
            x = jnp.concatenate([filled(v.astype(jnp.bfloat16)) for v in parts(lined, start)], axis=0)
            re, im = [filled(v).T[:height] for v in parts(mine, start)]
            both = jnp.concatenate([jnp.concatenate([re, im], axis=1), jnp.concatenate([im, -re], axis=1)], axis=0)
            result = jnp.dot(both.astype(jnp.bfloat16), x, preferred_element_type=jnp.float32) * scale
            out_ref[k, :, 0:inputs] = result[:height, :inputs]
            out_ref[k, :, inputs : 2 * inputs] = result[height:, :inputs]


def turned_gram(buf, channels, height, scale):
    peers, groups, steps, rows, _ = buf.shape
    inputs = groups * steps * GROUP
    packs = LANES // (2 * channels)
    depth = 2 * peers * packs * rows // GROUP
    some = math.gcd(channels, 4)
    which = lax.axis_index("tm").astype(jnp.int32).reshape(1)
    return pl.pallas_call(
        functools.partial(turned_gram_kernel, scale, channels),
        out_shape=jax.ShapeDtypeStruct((channels, height, 2 * inputs), jnp.float32),
        grid_spec=pltpu.PrefetchScalarGridSpec(
            num_scalar_prefetch=1,
            grid=(peers + channels // some,),
            in_specs=[pl.BlockSpec((1, groups, steps, rows, LANES), lambda i, w: (jnp.minimum(i, peers - 1), 0, 0, 0, 0))],
            out_specs=pl.BlockSpec((some, height, 2 * inputs), lambda i, w: (jnp.maximum(i - peers, 0), 0, 0)),
            scratch_shapes=[
                pltpu.VMEM((-(-inputs // LANES), channels * depth, LANES), jnp.float32),
                pltpu.VMEM((-(-height // LANES), channels * depth, LANES), jnp.float32),
            ],
        ),
        name="turned_gram",
    )(which, buf)


def shards(samples, delays, taps):
    channels = taps.shape[1]
    local_inputs, _, shard_len = samples.shape
    groups, peers = lax.axis_size("inp"), lax.axis_size("tm")
    inputs = local_inputs * groups
    spectra = shard_len // channels
    mine = channels // groups
    packs = LANES // (2 * mine)
    sent = front(samples, delays, taps)
    direct = local_inputs % GROUP == 0 and sent.shape[2] % 16 == 0 and groups & (groups - 1) == 0
    if direct and (inputs // peers) % local_inputs == 0:
        return turned_gram(exchange(sent), mine, inputs // peers, 1.0 / (spectra * peers))
    turned = lax.all_to_all(sent, "inp", split_axis=0, concat_axis=0, tiled=True)
    steps = turned.shape[1]
    turned = turned.reshape(groups, steps, spectra // packs, GROUP, packs, 2, mine)
    turned = turned.transpose(6, 5, 4, 2, 0, 1, 3).reshape(mine, 2 * spectra, groups, steps * GROUP)
    turned = turned[..., :local_inputs].reshape(mine, 2 * spectra, inputs)
    gathered = lax.all_gather(turned, "tm", axis=0, tiled=False)
    return gram(gathered, inputs // peers, 1.0 / (spectra * peers))


def solution(mesh):
    in_specs = (P("inp", None, "tm"), P("inp"), P())
    out_specs = P("inp", "tm", None)
    return jax.shard_map(shards, mesh=mesh, in_specs=in_specs, out_specs=out_specs, check_vma=False)
```
